256 devices in a mesh: row: 16 (over z, y_hi), col: 16 (over y_lo, x, core).
Axes of the slice: x: 4, y: 4 (y_hi: 2, y_lo: 2; y = y_hi * 2 + y_lo), z: 8, core: 2. Of those that a mesh axis runs over, the one named last changes fastest.
Arguments:
- amplitudes: bfloat16 [2048, 32768], P('row', 'col'), may hold values from -6 to 6
- amp_mask: int32 [64, 128], P('row', 'col'), may hold values from 0 to 1, as said below
- integrals: bfloat16 [16384, 32768], P('row', 'col'), may hold values from -0.0625 to 0.0625
- int_mask: int32 [64, 128], P('row', 'col'), may hold values 0 or 1
- occ_energy: float32 [2048], P('col'), may hold values from -1.5 to -0.5
- vir_energy: float32 [16384], P('row'), may hold values from 0.5 to 1.5
Outputs:
- residual: bfloat16 [2048, 16384], P('col', 'row')
The draws below stay inside these ranges and needn't reach their ends.
Inputs may be any that keep to these rules, and one draw needn't show every extreme that they name: In every row of amp_mask, each aligned group of 8 consecutive entries holds exactly 4 ones.
All inputs are finite; a program needn't handle non-finite values. No bound on the sum of `int_mask` on one device may be relied on, other than what follows from the above.
Results may differ from the reference program's by a relative error of at most 0.001.
Values may be sent and summed in bfloat16 or wider, within the bound.
A program may use at most 64 MiB of HBM per device.

```python
import jax
import jax.numpy as jnp
from jax import lax

TILE = 256
IJ_BLK = 32
GRP = 8
AB = 16384
CD = 32768
IJ = 2048


def draw_amp_mask(key, part):
    nrow = IJ // IJ_BLK
    ngroup = CD // TILE // GRP
    scores = jax.random.randint(jax.random.fold_in(key, 17), (nrow, ngroup, GRP), 0, 2 ** 20)
    distinct = scores * GRP + jnp.arange(GRP, dtype=jnp.int32)[None, None, :]
    order = jnp.argsort(distinct, axis=2)
    ranks = jnp.argsort(order, axis=2)
    return (ranks < GRP // 2).astype(jnp.int32).reshape(nrow, ngroup * GRP)


def set_ends(drawn, stream_key, low, high):
    longest = drawn.shape.index(max(drawn.shape))
    spots = []
    for shift in (0, 1):
        where = [jax.random.randint(jax.random.fold_in(stream_key, axis), (), 0, length) for axis, length in enumerate(drawn.shape)]
        where[longest] = (where[longest] + shift) % drawn.shape[longest]
        spots.append(tuple(where))
    return drawn.at[spots[0]].set(low).at[spots[1]].set(high)


def with_spikes(array, key, source, target, shards_of, factor):
    owner, partner = [(jnp.arange(array.shape[dim]) // (array.shape[dim] // shards_of)).reshape([-1 if axis == dim else 1 for axis in range(array.ndim)]) for dim in (source, target)]
    chosen = jax.random.permutation(key, shards_of)[partner]
    strong = (owner == chosen) | (owner == (partner + shards_of // 2) % shards_of)
    return jnp.where(strong, factor * array, array)


def block_scale(key, shape, shards, smallest, high):
    loudness, own = 1.0, jax.random.fold_in(key, 6)
    for axis_at, blocks in shards:
        heights = jnp.exp(jax.random.uniform(jax.random.fold_in(own, axis_at), (blocks,), jnp.float32, smallest / len(shards), high / len(shards)))
        loudness = loudness * jnp.repeat(heights, shape[axis_at] // blocks).reshape([-1 if axis == axis_at else 1 for axis in range(len(shape))])
    return loudness


def centred(key, dims, deviation, bound, pieces=(), kind=jnp.bfloat16):
    result = deviation * jax.random.normal(key, dims, jnp.float32)
    if pieces:
        result = result * block_scale(key, dims, pieces, -0.22, 0.18)
    return jnp.clip(result, -bound, bound).astype(kind)


def noise_with(key, dims, scale, reach, split, heavy, held_as=jnp.bfloat16):
    result = scale * jax.random.normal(key, dims, jnp.float32)
    if split:
        result = result * block_scale(key, dims, split, -0.22, 0.18)
    return jnp.clip(with_spikes(result, jax.random.fold_in(key, 3), *heavy), -reach, reach).astype(held_as)


def setup_inputs(seed: int = 0) -> dict:
    key_of = jax.random.split(jax.random.key(seed), 7)
    amplitudes = noise_with(key_of[0], (IJ, CD), 1.0, 6.0, ((0, 16), (1, 16)), (1, 0, 16, 2.0))
    amp_mask = draw_amp_mask(jax.random.fold_in(key_of[6], 71), 0)
    integrals = centred(key_of[2], (AB, CD), (CD // 4) ** -0.5, 0.0625, ((0, 16), (1, 16)))
    int_mask = set_ends((jax.random.randint(key_of[3], (AB // TILE, CD // TILE), 0, 2) < 1).astype(jnp.int32), jax.random.fold_in(key_of[3], 1), 0, 1)
    occ_energy = jnp.clip(-1.5 + 1.0 * jax.random.uniform(key_of[4], (IJ,), jnp.float32) ** block_scale(key_of[4], (IJ,), ((0, 16),), -0.2, 0.2), -1.5, -0.5)
    vir_energy = jnp.clip(0.5 + 1.0 * jax.random.uniform(key_of[5], (AB,), jnp.float32) ** block_scale(key_of[5], (AB,), ((0, 16),), -0.2, 0.2), 0.5, 1.5)
    return dict(amplitudes=amplitudes, amp_mask=amp_mask, integrals=integrals, int_mask=int_mask, occ_energy=occ_energy, vir_energy=vir_energy)


def reference(amplitudes, amp_mask, integrals, int_mask, occ_energy, vir_energy):
    amp_keep = jnp.repeat(jnp.repeat(amp_mask, IJ_BLK, axis=0), TILE, axis=1)
    amp_used = jnp.where(amp_keep == 1, amplitudes, jnp.zeros_like(amplitudes))

    def tile_rows(args):
        block, keep = args
        keep_cols = jnp.repeat(keep, TILE)
        used = jnp.where(keep_cols[None, :] == 1, block, jnp.zeros_like(block))
        return jnp.dot(amp_used, used.T, preferred_element_type=jnp.float32)

    blocks = integrals.reshape(AB // TILE, TILE, CD)
    parts = lax.map(tile_rows, (blocks, int_mask))
    ladder = jnp.transpose(parts, (1, 0, 2)).reshape(IJ, AB)
    denom = vir_energy[None, :] - occ_energy[:, None]
    return (ladder / denom).astype(jnp.bfloat16)
```

```python
import jax
import jax.numpy as jnp
from jax import lax
from jax.experimental import pallas as pl
from jax.experimental.pallas import tpu as pltpu
from jax.sharding import PartitionSpec as P

MESH = pl.DeviceIdType.MESH
TILE = 256
BLK = 32
KEPT = 4
NT = 8
NZ, NX = 8, 4
HALF = 64
CODE = 8 * HALF
PIECE = CODE + 16
ICH = 4


def kernel(amp_hbm, am, int_hbm, im, occ, vir, out,
           amp_v, int_v, own, pieces, dec, int_t, part, relay, roots, rows_in,
           amp_sem, int_sem, own_send, copy_sem, a_send, a_recv,
           t_send, t_recv, p_send, y_send, r1_recv, r2_recv, r3_recv):
    row, col = lax.axis_index("row"), lax.axis_index("col")
    z, yh = row // 2, lax.rem(row, 2)
    k, x, yl = lax.rem(col, 2), lax.rem(col // 2, NX), col // (2 * NX)
    z_up, z_dn = lax.rem(z + 1, NZ) * 2 + yh, lax.rem(z + NZ - 1, NZ) * 2 + yh
    x_up = (yl * NX + lax.rem(x + 1, NX)) * 2 + k
    x_dn = (yl * NX + lax.rem(x + NX - 1, NX)) * 2 + k
    core_other = (row, (yl * NX + x) * 2 + 1 - k)
    y_other = (row, ((1 - yl) * NX + x) * 2 + k)
    far_row = z * 2 + 1 - yh
    chip_col = (yl * NX + x) * 2

    def remote(src, dst, send, recv, device):
        return pltpu.make_async_remote_copy(
            src_ref=src, dst_ref=dst, send_sem=send, recv_sem=recv,
            device_id=device, device_id_type=MESH)

    amp_in = pltpu.make_async_copy(amp_hbm, amp_v, amp_sem)
    amp_in.start()
    width = NT * TILE // ICH
    int_in = [pltpu.make_async_copy(int_hbm.at[:, pl.ds(i * width, width)],
                                    int_v.at[:, pl.ds(i * width, width)], int_sem.at[i])
              for i in range(ICH)]
    for c in int_in:
        c.start()

    barrier = pltpu.get_barrier_semaphore()
    for device in ((z_up, col), (z_dn, col), (row, x_up), (row, x_dn), y_other, core_other,
                   (far_row, chip_col), (far_row, chip_col + 1)):
        pl.semaphore_signal(barrier, inc=1, device_id=device, device_id_type=MESH)

    amp_in.wait()
    row_id = lax.broadcasted_iota(jnp.int32, (16, 128), 0)
    for g in range(2):
        codes = jnp.zeros((16, 128), jnp.int32)
        for q in range(2):
            b = g * 2 + q
            count, code = jnp.int32(0), []
            for j in range(NT):
                m = am[b, j]
                count = count + m
                code.append(m * count)
                codes = jnp.where(row_id == q * NT + j, code[j], codes)
            for s in range(KEPT):
                for l in range(2):
                    acc = jnp.zeros((BLK, 128), jnp.bfloat16)
                    for j in range(s, s + KEPT + 1):
                        tile = amp_v[b * BLK:(b + 1) * BLK, j * TILE + l * 128:j * TILE + l * 128 + 128]
                        acc = jnp.where(code[j] == s + 1, tile, acc)
                    at = (s * 2 + l) * HALF + q * BLK
                    own[g, at:at + BLK, :] = acc
        own[g, CODE:CODE + 16, :] = codes.astype(jnp.float32).astype(jnp.bfloat16)

    pl.semaphore_wait(barrier, 8)

    far = [remote(own.at[g], pieces.at[0, g, k], own_send.at[0, g], a_recv.at[0, g, k],
                  (far_row, chip_col + yh)) for g in range(2)]
    near = [remote(own.at[g], pieces.at[0, g, k], own_send.at[1, g], a_recv.at[0, g, k],
                   core_other) for g in range(2)]
    keep = [pltpu.make_async_copy(own.at[g], pieces.at[0, g, k], a_recv.at[0, g, k])
            for g in range(2)]
    for g in range(2):
        far[g].start()

    @pl.when(k != yh)
    def _():
        for g in range(2):
            near[g].start()

    @pl.when(k == yh)
    def _():
        for g in range(2):
            keep[g].start()

    def turned(i, device):
        part_rows = pl.ds(pl.multiple_of(k * (NT * TILE) + i * width, width), width)
        return remote(int_t.at[part_rows], int_t.at[part_rows], t_send.at[i], t_recv.at[i], device)

    for i in range(ICH):
        int_in[i].wait()
        for jj in range(width // TILE):
            j = i * (width // TILE) + jj
            for a in range(4):
                tile = int_v[a * TILE:(a + 1) * TILE, j * TILE:(j + 1) * TILE]
                tile = jnp.where(im[a, j] != 0, tile, jnp.zeros_like(tile))
                at = pl.multiple_of(k * (NT * TILE) + j * TILE, TILE)
                int_t[pl.ds(at, TILE), a * TILE:(a + 1) * TILE] = tile.T
        turned(i, core_other).start()

    def forward(s, h):
        for g in range(2):
            to = (z_up, col) if g == 0 else (z_dn, col)
            remote(pieces.at[s, g, h], pieces.at[s, g, h], a_send.at[s, g, h],
                   a_recv.at[s, g, h], to).wait_recv()

            @pl.when(s + 1 < NZ)
            def _():
                after = lax.rem(s + 1, NZ)
                remote(pieces.at[s, g, h], pieces.at[after, g, h], a_send.at[s, g, h],
                       a_recv.at[after, g, h], to).start()

    forward(0, 0)
    for i in range(ICH):
        turned(i, core_other).wait_recv()

    def root_of(s, g):
        zs = lax.rem(z + NZ - s, NZ) if g == 0 else lax.rem(z + s, NZ)
        xr, yr = lax.rem(zs, NX), zs // NX
        return lax.rem(x + NX - xr, NX), yr

    def halves(s, g, w):
        return part.at[s, pl.ds(g * HALF + w * BLK, BLK), :]

    def compute(s):
        def spread(gh, _):
            g, h = gh // 2, lax.rem(gh, 2)
            for q in range(2):
                for j in range(NT):
                    code = jnp.broadcast_to(
                        pieces[s, g, h, CODE + q * NT + j:CODE + q * NT + j + 1, :], (BLK, 128))
                    for l in range(2):
                        acc = jnp.zeros((BLK, 128), jnp.bfloat16)
                        for t in range(max(0, j - KEPT), min(j, KEPT - 1) + 1):
                            at = (t * 2 + l) * HALF + q * BLK
                            acc = jnp.where(code == jnp.bfloat16(t + 1),
                                            pieces[s, g, h, at:at + BLK, :], acc)
                        to_row = pl.multiple_of(g * HALF + q * BLK, BLK)
                        to_col = pl.multiple_of(h * NT * TILE + j * TILE + l * 128, 128)
                        dec[pl.ds(to_row, BLK), pl.ds(to_col, 128)] = acc
            return 0

        lax.fori_loop(0, 4, spread, 0)
        for n in range(4):
            part[s, :, n * TILE:(n + 1) * TILE] = lax.dot_general(
                dec[...], int_t[:, n * TILE:(n + 1) * TILE], (((1,), (0,)), ((), ())),
                preferred_element_type=jnp.float32)

    def send_half(s, g, w, dst, recv, device):
        return remote(halves(s, g, w), dst, p_send.at[s, g, w], recv, device)

    def first(s):
        for g in range(2):
            d, yr = root_of(s, g)
            u, v = s * 2 + g, g * 2 + yr

            @pl.when(d == 2)
            def _():
                send_half(s, g, 0, relay.at[u], r1_recv.at[u], (row, x_dn)).start()
                send_half(s, g, 1, relay.at[u], r1_recv.at[u], (row, x_up)).start()

            @pl.when(d == 1)
            def _():
                send_half(s, g, 1, roots.at[v, 0, 1], r2_recv.at[v, 0, 1], (row, x_dn)).start()

            @pl.when(d == 3)
            def _():
                send_half(s, g, 0, roots.at[v, 1, 0], r2_recv.at[v, 1, 0], (row, x_up)).start()

    def second(s):
        for g in range(2):
            d, yr = root_of(s, g)
            u, v = s * 2 + g, g * 2 + yr

            @pl.when(d == 1)
            def _():
                send_half(s, g, 0, relay.at[u], r1_recv.at[u], (row, x_dn)).wait_recv()
                halves(s, g, 0)[...] += relay[u]
                send_half(s, g, 0, roots.at[v, 0, 0], r2_recv.at[v, 0, 0], (row, x_dn)).start()

            @pl.when(d == 3)
            def _():
                send_half(s, g, 1, relay.at[u], r1_recv.at[u], (row, x_up)).wait_recv()
                halves(s, g, 1)[...] += relay[u]
                send_half(s, g, 1, roots.at[v, 1, 1], r2_recv.at[v, 1, 1], (row, x_up)).start()

    def cross(s, g):
        whole = part.at[s, pl.ds(g * HALF, HALF), :]
        return remote(whole, rows_in.at[g], y_send.at[s, g], r3_recv.at[g], y_other)

    def third(s):
        for g in range(2):
            d, yr = root_of(s, g)
            v = g * 2 + yr

            @pl.when(d == 0)
            def _():
                for w in range(2):
                    for side in range(2):
                        send_half(s, g, w, roots.at[v, side, w], r2_recv.at[v, side, w],
                                  (row, x_dn)).wait_recv()
                    halves(s, g, w)[...] += roots[v, 0, w] + roots[v, 1, w]

                @pl.when(yr != yl)
                def _():
                    cross(s, g).start()

    def fourth(s):
        for g in range(2):
            d, yr = root_of(s, g)

            @pl.when(jnp.logical_and(d == 0, yr == yl))
            def _():
                cross(s, g).wait_recv()
                occ_col = jnp.broadcast_to(occ[...], (128, 128)).T
                for n in range(8):
                    cols = slice(n * 128, (n + 1) * 128)
                    total = part[s, g * HALF:(g + 1) * HALF, cols] + rows_in[g, :, cols]
                    denom = vir[:, cols] - occ_col[g * HALF:(g + 1) * HALF, :]
                    out[g * HALF:(g + 1) * HALF, cols] = (total / denom).astype(jnp.bfloat16)

    def step(t, _):
        @pl.when(t < NZ)
        def _():
            forward(t, 1)
            compute(t)
            first(t)

        @pl.when(t + 1 < NZ)
        def _():
            forward(t + 1, 0)

        @pl.when(jnp.logical_and(t >= 1, t - 1 < NZ))
        def _():
            second(t - 1)

        @pl.when(jnp.logical_and(t >= 2, t - 2 < NZ))
        def _():
            third(t - 2)

        @pl.when(t >= 3)
        def _():
            fourth(t - 3)

        return 0

    lax.fori_loop(0, NZ + 3, step, 0)

    for g in range(2):
        far[g].wait_send()

    @pl.when(k != yh)
    def _():
        for g in range(2):
            near[g].wait_send()

    for i in range(ICH):
        turned(i, core_other).wait_send()

    def drain(s, _):
        for g in range(2):
            @pl.when(s + 1 < NZ)
            def _():
                for h in range(2):
                    remote(pieces.at[s, g, h], pieces.at[s, g, h], a_send.at[s, g, h],
                           a_recv.at[s, g, h], (z_up, col)).wait_send()

            d, yr = root_of(s, g)

            @pl.when(d != 0)
            def _():
                for w in range(2):
                    send_half(s, g, w, relay.at[0], r1_recv.at[0], (row, x_dn)).wait_send()

            @pl.when(jnp.logical_and(d == 0, yr != yl))
            def _():
                cross(s, g).wait_send()
        return 0

    lax.fori_loop(0, NZ, drain, 0)


def body(amplitudes, amp_mask, integrals, int_mask, occ_energy, vir_energy):
    nij, ncd = amplitudes.shape
    nab = integrals.shape[0]
    dma = pltpu.SemaphoreType.DMA
    vmem = pl.BlockSpec(memory_space=pltpu.VMEM)
    smem = pl.BlockSpec(memory_space=pltpu.SMEM)
    hbm = pl.BlockSpec(memory_space=pl.ANY)
    return pl.pallas_call(
        kernel,
        out_shape=jax.ShapeDtypeStruct((nij, nab), jnp.bfloat16),
        in_specs=[hbm, smem, hbm, smem, vmem, vmem],
        out_specs=vmem,
        scratch_shapes=[
            pltpu.VMEM((nij, ncd), jnp.bfloat16),
            pltpu.VMEM((nab, ncd), jnp.bfloat16),
            pltpu.VMEM((2, PIECE, 128), jnp.bfloat16),
            pltpu.VMEM((NZ, 2, 2, PIECE, 128), jnp.bfloat16),
            pltpu.VMEM((nij, 2 * ncd), jnp.bfloat16),
            pltpu.VMEM((2 * ncd, nab), jnp.bfloat16),
            pltpu.VMEM((NZ, nij, nab), jnp.float32),
            pltpu.VMEM((2 * NZ, BLK, nab), jnp.float32),
            pltpu.VMEM((4, 2, 2, BLK, nab), jnp.float32),
            pltpu.VMEM((2, HALF, nab), jnp.float32),
            dma, dma((ICH,)), dma((2, 2)), dma, dma((NZ, 2, 2)), dma((NZ, 2, 2)),
            dma((ICH,)), dma((ICH,)), dma((NZ, 2, 2)), dma((NZ, 2)),
            dma((2 * NZ,)), dma((4, 2, 2)), dma((2,)),
        ],
        compiler_params=pltpu.CompilerParams(
            collective_id=0, has_side_effects=True, vmem_limit_bytes=60 * 1024 * 1024),
    )(amplitudes, amp_mask, integrals, int_mask, occ_energy[None, :], vir_energy[None, :])


def solution(mesh):
    return jax.shard_map(
        body,
        mesh=mesh,
        in_specs=(
            P("row", "col"),
            P("row", "col"),
            P("row", "col"),
            P("row", "col"),
            P("col"),
            P("row"),
        ),
        out_specs=P("col", "row"),
        check_vma=False,
    )
```

```python
import jax
import jax.numpy as jnp
from jax import lax
from jax.experimental import pallas as pl
from jax.experimental.pallas import tpu as pltpu
from jax.sharding import PartitionSpec as P

MESH = pl.DeviceIdType.MESH
TILE = 256
BLK = 32
KEPT = 4
NT = 8
NZ, NX = 8, 4
HALF = 64
CODE = 8 * HALF
PIECE = CODE + 16
NEAR = 3
LAG = (2, 4, 6)
ICH = 4


def kernel(amp_hbm, am, int_hbm, im, occ, vir, out,
           amp_v, int_v, own, pieces, dec, int_t, part, relay, roots, rows_in,
           amp_sem, int_sem, own_send, a_send, a_recv, far_send,
           t_send, t_recv, p_send, y_send, r1_recv, r2_recv, r3_recv):
    row, col = lax.axis_index("row"), lax.axis_index("col")
    z, yh = row // 2, lax.rem(row, 2)
    k, x, yl = lax.rem(col, 2), lax.rem(col // 2, NX), col // (2 * NX)
    z_up, z_dn = lax.rem(z + 1, NZ) * 2 + yh, lax.rem(z + NZ - 1, NZ) * 2 + yh
    x_up = (yl * NX + lax.rem(x + 1, NX)) * 2 + k
    x_dn = (yl * NX + lax.rem(x + NX - 1, NX)) * 2 + k
    core_other = (row, (yl * NX + x) * 2 + 1 - k)
    y_other = (row, ((1 - yl) * NX + x) * 2 + k)
    far_row = z * 2 + 1 - yh
    chip_col = (yl * NX + x) * 2

    def remote(src, dst, send, recv, device):
        return pltpu.make_async_remote_copy(
            src_ref=src, dst_ref=dst, send_sem=send, recv_sem=recv,
            device_id=device, device_id_type=MESH)

    amp_in = pltpu.make_async_copy(amp_hbm, amp_v, amp_sem)
    amp_in.start()
    width = NT * TILE // ICH
    int_in = [pltpu.make_async_copy(int_hbm.at[:, pl.ds(i * width, width)],
                                    int_v.at[:, pl.ds(i * width, width)], int_sem.at[i])
              for i in range(ICH)]
    for c in int_in:
        c.start()

    barrier = pltpu.get_barrier_semaphore()
    for device in ((z_up, col), (z_dn, col), (row, x_up), (row, x_dn), y_other, core_other,
                   (far_row, chip_col), (far_row, chip_col + 1)):
        pl.semaphore_signal(barrier, inc=1, device_id=device, device_id_type=MESH)

    amp_in.wait()
    row_id = lax.broadcasted_iota(jnp.int32, (16, 128), 0)
    for g in range(2):
        codes = jnp.zeros((16, 128), jnp.int32)
        for q in range(2):
            b = g * 2 + q
            count, code = jnp.int32(0), []
            for j in range(NT):
                m = am[b, j]
                count = count + m
                code.append(m * count)
                codes = jnp.where(row_id == q * NT + j, code[j], codes)
            for s in range(KEPT):
                for l in range(2):
                    acc = jnp.zeros((BLK, 128), jnp.bfloat16)
                    for j in range(s, s + KEPT + 1):
                        tile = amp_v[b * BLK:(b + 1) * BLK, j * TILE + l * 128:j * TILE + l * 128 + 128]
                        acc = jnp.where(code[j] == s + 1, tile, acc)
                    at = (s * 2 + l) * HALF + q * BLK
                    own[g, at:at + BLK, :] = acc
        own[g, CODE:CODE + 16, :] = codes.astype(jnp.float32).astype(jnp.bfloat16)

    pl.semaphore_wait(barrier, 8)

    far = [remote(own.at[g], pieces.at[0, g, k], own_send.at[0, g], a_recv.at[0, g, k],
                  (far_row, chip_col + yh)) for g in range(2)]
    near = [remote(own.at[g], pieces.at[0, g, k], own_send.at[1, g], a_recv.at[0, g, k],
                   core_other) for g in range(2)]
    keep = [pltpu.make_async_copy(own.at[g], pieces.at[0, g, k], a_recv.at[0, g, k])
            for g in range(2)]
    for g in range(2):
        far[g].start()

    @pl.when(k != yh)
    def _():
        for g in range(2):
            near[g].start()

    @pl.when(k == yh)
    def _():
        for g in range(2):
            keep[g].start()

    def onward(src, s, g, h):
        to = (z_up, col) if g == 0 else (z_dn, col)
        after = lax.rem(s + 1, NZ)
        return remote(src, pieces.at[after, g, h], a_send.at[s, g, h], a_recv.at[after, g, h], to)

    def over(s, g, h):
        return remote(pieces.at[s, g, h], pieces.at[s, g, h], far_send.at[s, g, h],
                      a_recv.at[s, g, h], (far_row, col))

    def arrived(s, g, h):
        remote(pieces.at[s, g, h], pieces.at[s, g, h], a_send.at[s, g, h], a_recv.at[s, g, h],
               (z_up, col)).wait_recv()

    home = k == yh

    def goes_on(s):
        return jnp.logical_and(s + 1 < NZ, jnp.logical_or(home, s >= NEAR))

    def goes_over(s):
        return jnp.logical_and(home, jnp.logical_and(s >= 1, s <= NEAR))

    def forward(s, h):
        for g in range(2):
            arrived(s, g, h)

            @pl.when(goes_on(s))
            def _():
                onward(pieces.at[s, g, h], s, g, h).start()

            @pl.when(goes_over(s))
            def _():
                over(s, g, h).start()

    @pl.when(home)
    def _():
        for g in range(2):
            onward(own.at[g], 0, g, k).start()

    def turned(i, device):
        part_rows = pl.ds(pl.multiple_of(k * (NT * TILE) + i * width, width), width)
        return remote(int_t.at[part_rows], int_t.at[part_rows], t_send.at[i], t_recv.at[i], device)

    for i in range(ICH):
        int_in[i].wait()
        for jj in range(width // TILE):
            j = i * (width // TILE) + jj
            for a in range(4):
                tile = int_v[a * TILE:(a + 1) * TILE, j * TILE:(j + 1) * TILE]
                tile = jnp.where(im[a, j] != 0, tile, jnp.zeros_like(tile))
                at = pl.multiple_of(k * (NT * TILE) + j * TILE, TILE)
                int_t[pl.ds(at, TILE), a * TILE:(a + 1) * TILE] = tile.T
        turned(i, core_other).start()
        if i == 0:
            @pl.when(home)
            def _():
                for g in range(2):
                    arrived(0, g, 1 - k)
                    onward(pieces.at[0, g, 1 - k], 0, g, 1 - k).start()

    @pl.when(home)
    def _():
        for g in range(2):
            arrived(0, g, k)

    @pl.when(jnp.logical_not(home))
    def _():
        forward(0, 0)
        forward(0, 1)

    for i in range(ICH):
        turned(i, core_other).wait_recv()

    def root_of(s, g):
        zs = lax.rem(z + NZ - s, NZ) if g == 0 else lax.rem(z + s, NZ)
        xr, yr = lax.rem(zs, NX), zs // NX
        return lax.rem(x + NX - xr, NX), yr

    def halves(s, g, w):
        return part.at[s, pl.ds(g * HALF + w * BLK, BLK), :]

    def compute(s):
        def spread(gh, _):
            g, h = gh // 2, lax.rem(gh, 2)
            for q in range(2):
                for j in range(NT):
                    code = jnp.broadcast_to(
                        pieces[s, g, h, CODE + q * NT + j:CODE + q * NT + j + 1, :], (BLK, 128))
                    for l in range(2):
                        acc = jnp.zeros((BLK, 128), jnp.bfloat16)
                        for t in range(max(0, j - KEPT), min(j, KEPT - 1) + 1):
                            at = (t * 2 + l) * HALF + q * BLK
                            acc = jnp.where(code == jnp.bfloat16(t + 1),
                                            pieces[s, g, h, at:at + BLK, :], acc)
                        to_row = pl.multiple_of(g * HALF + q * BLK, BLK)
                        to_col = pl.multiple_of(h * NT * TILE + j * TILE + l * 128, 128)
                        dec[pl.ds(to_row, BLK), pl.ds(to_col, 128)] = acc
            return 0

        lax.fori_loop(0, 4, spread, 0)
        for n in range(4):
            part[s, :, n * TILE:(n + 1) * TILE] = lax.dot_general(
                dec[...], int_t[:, n * TILE:(n + 1) * TILE], (((1,), (0,)), ((), ())),
                preferred_element_type=jnp.float32)

    def send_half(s, g, w, dst, recv, device):
        return remote(halves(s, g, w), dst, p_send.at[s, g, w], recv, device)

    def first(s):
        for g in range(2):
            d, yr = root_of(s, g)
            u, v = s * 2 + g, g * 2 + yr

            @pl.when(d == 2)
            def _():
                send_half(s, g, 0, relay.at[u], r1_recv.at[u], (row, x_dn)).start()
                send_half(s, g, 1, relay.at[u], r1_recv.at[u], (row, x_up)).start()

            @pl.when(d == 1)
            def _():
                send_half(s, g, 1, roots.at[v, 0, 1], r2_recv.at[v, 0, 1], (row, x_dn)).start()

            @pl.when(d == 3)
            def _():
                send_half(s, g, 0, roots.at[v, 1, 0], r2_recv.at[v, 1, 0], (row, x_up)).start()

    def second(s):
        for g in range(2):
            d, yr = root_of(s, g)
            u, v = s * 2 + g, g * 2 + yr

            @pl.when(d == 1)
            def _():
                send_half(s, g, 0, relay.at[u], r1_recv.at[u], (row, x_dn)).wait_recv()
                halves(s, g, 0)[...] += relay[u]
                send_half(s, g, 0, roots.at[v, 0, 0], r2_recv.at[v, 0, 0], (row, x_dn)).start()

            @pl.when(d == 3)
            def _():
                send_half(s, g, 1, relay.at[u], r1_recv.at[u], (row, x_up)).wait_recv()
                halves(s, g, 1)[...] += relay[u]
                send_half(s, g, 1, roots.at[v, 1, 1], r2_recv.at[v, 1, 1], (row, x_up)).start()

    def cross(s, g):
        whole = part.at[s, pl.ds(g * HALF, HALF), :]
        return remote(whole, rows_in.at[g], y_send.at[s, g], r3_recv.at[g], y_other)

    def third(s):
        for g in range(2):
            d, yr = root_of(s, g)
            v = g * 2 + yr

            @pl.when(d == 0)
            def _():
                for w in range(2):
                    for side in range(2):
                        send_half(s, g, w, roots.at[v, side, w], r2_recv.at[v, side, w],
                                  (row, x_dn)).wait_recv()
                    halves(s, g, w)[...] += roots[v, 0, w] + roots[v, 1, w]

                @pl.when(yr != yl)
                def _():
                    cross(s, g).start()

    def fourth(s):
        for g in range(2):
            d, yr = root_of(s, g)

            @pl.when(jnp.logical_and(d == 0, yr == yl))
            def _():
                cross(s, g).wait_recv()
                occ_col = jnp.broadcast_to(occ[...], (128, 128)).T
                for n in range(8):
                    cols = slice(n * 128, (n + 1) * 128)
                    total = part[s, g * HALF:(g + 1) * HALF, cols] + rows_in[g, :, cols]
                    denom = vir[:, cols] - occ_col[g * HALF:(g + 1) * HALF, :]
                    out[g * HALF:(g + 1) * HALF, cols] = (total / denom).astype(jnp.bfloat16)

    def step(t, _):
        @pl.when(t < NZ)
        def _():
            compute(t)
            first(t)

        @pl.when(t + 1 < NZ)
        def _():
            forward(t + 1, 0)

        for lag, job in zip(LAG, (second, third, fourth)):
            @pl.when(jnp.logical_and(t >= lag, t - lag < NZ))
            def _():
                job(t - lag)

        @pl.when(t + 1 < NZ)
        def _():
            forward(t + 1, 1)

        return 0

    lax.fori_loop(0, NZ + LAG[2], step, 0)

    for g in range(2):
        far[g].wait_send()

    @pl.when(k != yh)
    def _():
        for g in range(2):
            near[g].wait_send()

    for i in range(ICH):
        turned(i, core_other).wait_send()

    def drain(s, _):
        for g in range(2):
            @pl.when(goes_on(s))
            def _():
                for h in range(2):
                    onward(pieces.at[s, g, h], s, g, h).wait_send()

            @pl.when(goes_over(s))
            def _():
                for h in range(2):
                    over(s, g, h).wait_send()

            d, yr = root_of(s, g)

            @pl.when(d != 0)
            def _():
                for w in range(2):
                    send_half(s, g, w, relay.at[0], r1_recv.at[0], (row, x_dn)).wait_send()

            @pl.when(jnp.logical_and(d == 0, yr != yl))
            def _():
                cross(s, g).wait_send()
        return 0

    lax.fori_loop(0, NZ, drain, 0)


def body(amplitudes, amp_mask, integrals, int_mask, occ_energy, vir_energy):
    nij, ncd = amplitudes.shape
    nab = integrals.shape[0]
    dma = pltpu.SemaphoreType.DMA
    vmem = pl.BlockSpec(memory_space=pltpu.VMEM)
    smem = pl.BlockSpec(memory_space=pltpu.SMEM)
    hbm = pl.BlockSpec(memory_space=pl.ANY)
    return pl.pallas_call(
        kernel,
        out_shape=jax.ShapeDtypeStruct((nij, nab), jnp.bfloat16),
        in_specs=[hbm, smem, hbm, smem, vmem, vmem],
        out_specs=vmem,
        scratch_shapes=[
            pltpu.VMEM((nij, ncd), jnp.bfloat16),
            pltpu.VMEM((nab, ncd), jnp.bfloat16),
            pltpu.VMEM((2, PIECE, 128), jnp.bfloat16),
            pltpu.VMEM((NZ, 2, 2, PIECE, 128), jnp.bfloat16),
            pltpu.VMEM((nij, 2 * ncd), jnp.bfloat16),
            pltpu.VMEM((2 * ncd, nab), jnp.bfloat16),
            pltpu.VMEM((NZ, nij, nab), jnp.float32),
            pltpu.VMEM((2 * NZ, BLK, nab), jnp.float32),
            pltpu.VMEM((4, 2, 2, BLK, nab), jnp.float32),
            pltpu.VMEM((2, HALF, nab), jnp.float32),
            dma, dma((ICH,)), dma((2, 2)), dma((NZ, 2, 2)), dma((NZ, 2, 2)), dma((NZ, 2, 2)),
            dma((ICH,)), dma((ICH,)), dma((NZ, 2, 2)), dma((NZ, 2)),
            dma((2 * NZ,)), dma((4, 2, 2)), dma((2,)),
        ],
        compiler_params=pltpu.CompilerParams(
            collective_id=0, has_side_effects=True, vmem_limit_bytes=60 * 1024 * 1024),
    )(amplitudes, amp_mask, integrals, int_mask, occ_energy[None, :], vir_energy[None, :])


def solution(mesh):
    return jax.shard_map(
        body,
        mesh=mesh,
        in_specs=(
            P("row", "col"),
            P("row", "col"),
            P("row", "col"),
            P("row", "col"),
            P("col"),
            P("row"),
        ),
        out_specs=P("col", "row"),
        check_vma=False,
    )
```

```python
import jax
import jax.numpy as jnp
from jax import lax
from jax.experimental import pallas as pl
from jax.experimental.pallas import tpu as pltpu
from jax.sharding import PartitionSpec as P

MESH = pl.DeviceIdType.MESH
TILE = 256
BLK = 32
KEPT = 4
NT = 8
NZ, NX = 8, 4
HALF = 64
CODE = 8 * HALF
PIECE = CODE + 16
NEAR = 3
LAG = (2, 4, 6)
CUTS = ((0, 272), (272, 256))
ICH = 4


def kernel(amp_hbm, am, int_hbm, im, occ, vir, out,
           amp_v, int_v, own, pieces, dec, int_t, part, relay, roots, rows_in,
           amp_sem, int_sem, own_send, a_send, a_recv, far_send,
           t_send, t_recv, p_send, y_send, r1_recv, r2_recv, r3_recv):
    row, col = lax.axis_index("row"), lax.axis_index("col")
    z, yh = row // 2, lax.rem(row, 2)
    k, x, yl = lax.rem(col, 2), lax.rem(col // 2, NX), col // (2 * NX)
    z_up, z_dn = lax.rem(z + 1, NZ) * 2 + yh, lax.rem(z + NZ - 1, NZ) * 2 + yh
    x_up = (yl * NX + lax.rem(x + 1, NX)) * 2 + k
    x_dn = (yl * NX + lax.rem(x + NX - 1, NX)) * 2 + k
    core_other = (row, (yl * NX + x) * 2 + 1 - k)
    y_other = (row, ((1 - yl) * NX + x) * 2 + k)
    far_row = z * 2 + 1 - yh
    chip_col = (yl * NX + x) * 2

    def remote(src, dst, send, recv, device):
        return pltpu.make_async_remote_copy(
            src_ref=src, dst_ref=dst, send_sem=send, recv_sem=recv,
            device_id=device, device_id_type=MESH)

    amp_in = pltpu.make_async_copy(amp_hbm, amp_v, amp_sem)
    amp_in.start()
    width = NT * TILE // ICH
    int_in = [pltpu.make_async_copy(int_hbm.at[:, pl.ds(i * width, width)],
                                    int_v.at[:, pl.ds(i * width, width)], int_sem.at[i])
              for i in range(ICH)]
    for c in int_in:
        c.start()

    barrier = pltpu.get_barrier_semaphore()
    for device in ((z_up, col), (z_dn, col), (row, x_up), (row, x_dn), y_other, core_other,
                   (far_row, chip_col), (far_row, chip_col + 1)):
        pl.semaphore_signal(barrier, inc=1, device_id=device, device_id_type=MESH)

    amp_in.wait()
    row_id = lax.broadcasted_iota(jnp.int32, (16, 128), 0)
    for g in range(2):
        codes = jnp.zeros((16, 128), jnp.int32)
        for q in range(2):
            b = g * 2 + q
            count, code = jnp.int32(0), []
            for j in range(NT):
                m = am[b, j]
                count = count + m
                code.append(m * count)
                codes = jnp.where(row_id == q * NT + j, code[j], codes)
            for s in range(KEPT):
                for l in range(2):
                    acc = jnp.zeros((BLK, 128), jnp.bfloat16)
                    for j in range(s, s + KEPT + 1):
                        tile = amp_v[b * BLK:(b + 1) * BLK, j * TILE + l * 128:j * TILE + l * 128 + 128]
                        acc = jnp.where(code[j] == s + 1, tile, acc)
                    at = (s * 2 + l) * HALF + q * BLK
                    own[g, at:at + BLK, :] = acc
        own[g, CODE:CODE + 16, :] = codes.astype(jnp.float32).astype(jnp.bfloat16)

    pl.semaphore_wait(barrier, 8)

    def own_cut(g, u):
        return own.at[g, pl.ds(*CUTS[u]), :]

    def cut(s, g, h, u):
        return pieces.at[s, g, h, pl.ds(*CUTS[u]), :]

    def far(g, u):
        return remote(own_cut(g, u), cut(0, g, k, u), own_send.at[0, g, u],
                      a_recv.at[0, g, k, u], (far_row, chip_col + yh))

    def near(g, u):
        return remote(own_cut(g, u), cut(0, g, k, u), own_send.at[1, g, u],
                      a_recv.at[0, g, k, u], core_other)

    def keep(g, u):
        return pltpu.make_async_copy(own_cut(g, u), cut(0, g, k, u), a_recv.at[0, g, k, u])

    def onward(src, s, g, h, u):
        to = (z_up, col) if g == 0 else (z_dn, col)
        after = lax.rem(s + 1, NZ)
        return remote(src, cut(after, g, h, u), a_send.at[s, g, h, u], a_recv.at[after, g, h, u],
                      to)

    def over(s, g, h, u):
        return remote(cut(s, g, h, u), cut(s, g, h, u), far_send.at[s, g, h, u],
                      a_recv.at[s, g, h, u], (far_row, col))

    def arrived(s, g, h, u):
        remote(cut(s, g, h, u), cut(s, g, h, u), a_send.at[s, g, h, u], a_recv.at[s, g, h, u],
               (z_up, col)).wait_recv()

    home = k == yh
    each = [(u, g) for u in range(2) for g in range(2)]

    @pl.when(home)
    def _():
        for u, g in each:
            onward(own_cut(g, u), 0, g, k, u).start()

    @pl.when(k != yh)
    def _():
        for u, g in each:
            near(g, u).start()

    for u, g in each:
        far(g, u).start()

    @pl.when(home)
    def _():
        for u, g in each:
            keep(g, u).start()

    def goes_on(s):
        return jnp.logical_and(s + 1 < NZ, jnp.logical_or(home, s >= NEAR))

    def goes_over(s):
        return jnp.logical_and(home, jnp.logical_and(s >= 1, s <= NEAR))

    def forward(s, h):
        for u, g in each:
            arrived(s, g, h, u)

            @pl.when(goes_on(s))
            def _():
                onward(cut(s, g, h, u), s, g, h, u).start()

            @pl.when(goes_over(s))
            def _():
                over(s, g, h, u).start()

    def turned(i, device):
        part_rows = pl.ds(pl.multiple_of(k * (NT * TILE) + i * width, width), width)
        return remote(int_t.at[part_rows], int_t.at[part_rows], t_send.at[i], t_recv.at[i], device)

    for i in range(ICH):
        int_in[i].wait()
        for jj in range(width // TILE):
            j = i * (width // TILE) + jj
            for a in range(4):
                tile = int_v[a * TILE:(a + 1) * TILE, j * TILE:(j + 1) * TILE]
                tile = jnp.where(im[a, j] != 0, tile, jnp.zeros_like(tile))
                at = pl.multiple_of(k * (NT * TILE) + j * TILE, TILE)
                int_t[pl.ds(at, TILE), a * TILE:(a + 1) * TILE] = tile.T
        turned(i, core_other).start()
        if i == 0:
            @pl.when(home)
            def _():
                for u, g in each:
                    arrived(0, g, 1 - k, u)
                    onward(cut(0, g, 1 - k, u), 0, g, 1 - k, u).start()

    @pl.when(home)
    def _():
        for u, g in each:
            arrived(0, g, k, u)

    @pl.when(jnp.logical_not(home))
    def _():
        forward(0, 0)
        forward(0, 1)

    for i in range(ICH):
        turned(i, core_other).wait_recv()

    def root_of(s, g):
        zs = lax.rem(z + NZ - s, NZ) if g == 0 else lax.rem(z + s, NZ)
        xr, yr = lax.rem(zs, NX), zs // NX
        return lax.rem(x + NX - xr, NX), yr

    def halves(s, g, w):
        return part.at[s, pl.ds(g * HALF + w * BLK, BLK), :]

    def compute(s):
        def spread(gh, _):
            g, h = gh // 2, lax.rem(gh, 2)
            for q in range(2):
                for j in range(NT):
                    code = jnp.broadcast_to(
                        pieces[s, g, h, CODE + q * NT + j:CODE + q * NT + j + 1, :], (BLK, 128))
                    for l in range(2):
                        acc = jnp.zeros((BLK, 128), jnp.bfloat16)
                        for t in range(max(0, j - KEPT), min(j, KEPT - 1) + 1):
                            at = (t * 2 + l) * HALF + q * BLK
                            acc = jnp.where(code == jnp.bfloat16(t + 1),
                                            pieces[s, g, h, at:at + BLK, :], acc)
                        to_row = pl.multiple_of(g * HALF + q * BLK, BLK)
                        to_col = pl.multiple_of(h * NT * TILE + j * TILE + l * 128, 128)
                        dec[pl.ds(to_row, BLK), pl.ds(to_col, 128)] = acc
            return 0

        lax.fori_loop(0, 4, spread, 0)
        for n in range(4):
            part[s, :, n * TILE:(n + 1) * TILE] = lax.dot_general(
                dec[...], int_t[:, n * TILE:(n + 1) * TILE], (((1,), (0,)), ((), ())),
                preferred_element_type=jnp.float32)

    def send_half(s, g, w, dst, recv, device):
        return remote(halves(s, g, w), dst, p_send.at[s, g, w], recv, device)

    def first(s):
        for g in range(2):
            d, yr = root_of(s, g)
            u, v = s * 2 + g, g * 2 + yr

            @pl.when(d == 2)
            def _():
                send_half(s, g, 0, relay.at[u], r1_recv.at[u], (row, x_dn)).start()
                send_half(s, g, 1, relay.at[u], r1_recv.at[u], (row, x_up)).start()

            @pl.when(d == 1)
            def _():
                send_half(s, g, 1, roots.at[v, 0, 1], r2_recv.at[v, 0, 1], (row, x_dn)).start()

            @pl.when(d == 3)
            def _():
                send_half(s, g, 0, roots.at[v, 1, 0], r2_recv.at[v, 1, 0], (row, x_up)).start()

    def second(s):
        for g in range(2):
            d, yr = root_of(s, g)
            u, v = s * 2 + g, g * 2 + yr

            @pl.when(d == 1)
            def _():
                send_half(s, g, 0, relay.at[u], r1_recv.at[u], (row, x_dn)).wait_recv()
                halves(s, g, 0)[...] += relay[u]
                send_half(s, g, 0, roots.at[v, 0, 0], r2_recv.at[v, 0, 0], (row, x_dn)).start()

            @pl.when(d == 3)
            def _():
                send_half(s, g, 1, relay.at[u], r1_recv.at[u], (row, x_up)).wait_recv()
                halves(s, g, 1)[...] += relay[u]
                send_half(s, g, 1, roots.at[v, 1, 1], r2_recv.at[v, 1, 1], (row, x_up)).start()

    def cross(s, g):
        whole = part.at[s, pl.ds(g * HALF, HALF), :]
        return remote(whole, rows_in.at[g], y_send.at[s, g], r3_recv.at[g], y_other)

    def third(s):
        for g in range(2):
            d, yr = root_of(s, g)
            v = g * 2 + yr

            @pl.when(d == 0)
            def _():
                for w in range(2):
                    for side in range(2):
                        send_half(s, g, w, roots.at[v, side, w], r2_recv.at[v, side, w],
                                  (row, x_dn)).wait_recv()
                    halves(s, g, w)[...] += roots[v, 0, w] + roots[v, 1, w]

                @pl.when(yr != yl)
                def _():
                    cross(s, g).start()

    def fourth(s):
        for g in range(2):
            d, yr = root_of(s, g)

            @pl.when(jnp.logical_and(d == 0, yr == yl))
            def _():
                cross(s, g).wait_recv()
                occ_col = jnp.broadcast_to(occ[...], (128, 128)).T
                for n in range(8):
                    cols = slice(n * 128, (n + 1) * 128)
                    total = part[s, g * HALF:(g + 1) * HALF, cols] + rows_in[g, :, cols]
                    denom = vir[:, cols] - occ_col[g * HALF:(g + 1) * HALF, :]
                    out[g * HALF:(g + 1) * HALF, cols] = (total / denom).astype(jnp.bfloat16)

    def step(t, _):
        @pl.when(t < NZ)
        def _():
            compute(t)
            first(t)

        @pl.when(t + 1 < NZ)
        def _():
            forward(t + 1, 0)

        for lag, job in zip(LAG, (second, third, fourth)):
            @pl.when(jnp.logical_and(t >= lag, t - lag < NZ))
            def _():
                job(t - lag)

        @pl.when(t + 1 < NZ)
        def _():
            forward(t + 1, 1)

        return 0

    lax.fori_loop(0, NZ + LAG[2], step, 0)

    for u, g in each:
        far(g, u).wait_send()

    @pl.when(k != yh)
    def _():
        for u, g in each:
            near(g, u).wait_send()

    for i in range(ICH):
        turned(i, core_other).wait_send()

    def drain(s, _):
        for g in range(2):
            @pl.when(goes_on(s))
            def _():
                for h in range(2):
                    for u in range(2):
                        onward(cut(s, g, h, u), s, g, h, u).wait_send()

            @pl.when(goes_over(s))
            def _():
                for h in range(2):
                    for u in range(2):
                        over(s, g, h, u).wait_send()

            d, yr = root_of(s, g)

            @pl.when(d != 0)
            def _():
                for w in range(2):
                    send_half(s, g, w, relay.at[0], r1_recv.at[0], (row, x_dn)).wait_send()

            @pl.when(jnp.logical_and(d == 0, yr != yl))
            def _():
                cross(s, g).wait_send()
        return 0

    lax.fori_loop(0, NZ, drain, 0)


def body(amplitudes, amp_mask, integrals, int_mask, occ_energy, vir_energy):
    nij, ncd = amplitudes.shape
    nab = integrals.shape[0]
    dma = pltpu.SemaphoreType.DMA
    vmem = pl.BlockSpec(memory_space=pltpu.VMEM)
    smem = pl.BlockSpec(memory_space=pltpu.SMEM)
    hbm = pl.BlockSpec(memory_space=pl.ANY)
    return pl.pallas_call(
        kernel,
        out_shape=jax.ShapeDtypeStruct((nij, nab), jnp.bfloat16),
        in_specs=[hbm, smem, hbm, smem, vmem, vmem],
        out_specs=vmem,
        scratch_shapes=[
            pltpu.VMEM((nij, ncd), jnp.bfloat16),
            pltpu.VMEM((nab, ncd), jnp.bfloat16),
            pltpu.VMEM((2, PIECE, 128), jnp.bfloat16),
            pltpu.VMEM((NZ, 2, 2, PIECE, 128), jnp.bfloat16),
            pltpu.VMEM((nij, 2 * ncd), jnp.bfloat16),
            pltpu.VMEM((2 * ncd, nab), jnp.bfloat16),
            pltpu.VMEM((NZ, nij, nab), jnp.float32),
            pltpu.VMEM((2 * NZ, BLK, nab), jnp.float32),
            pltpu.VMEM((4, 2, 2, BLK, nab), jnp.float32),
            pltpu.VMEM((2, HALF, nab), jnp.float32),
            dma, dma((ICH,)), dma((2, 2, 2)), dma((NZ, 2, 2, 2)), dma((NZ, 2, 2, 2)),
            dma((NZ, 2, 2, 2)),
            dma((ICH,)), dma((ICH,)), dma((NZ, 2, 2)), dma((NZ, 2)),
            dma((2 * NZ,)), dma((4, 2, 2)), dma((2,)),
        ],
        compiler_params=pltpu.CompilerParams(
            collective_id=0, has_side_effects=True, vmem_limit_bytes=60 * 1024 * 1024),
    )(amplitudes, amp_mask, integrals, int_mask, occ_energy[None, :], vir_energy[None, :])


def solution(mesh):
    return jax.shard_map(
        body,
        mesh=mesh,
        in_specs=(
            P("row", "col"),
            P("row", "col"),
            P("row", "col"),
            P("row", "col"),
            P("col"),
            P("row"),
        ),
        out_specs=P("col", "row"),
        check_vma=False,
    )
```

```python
import jax
import jax.numpy as jnp
from jax import lax
from jax.experimental import pallas as pl
from jax.experimental.pallas import tpu as pltpu
from jax.sharding import PartitionSpec as P

MESH = pl.DeviceIdType.MESH
TILE = 256
BLK = 32
KEPT = 4
NT = 8
NZ, NX = 8, 4
HALF = 64
CODE = 8 * HALF
PIECE = CODE + 16
NEAR = 3
LAG = (2, 4, 6)
CUTS = ((0, 272), (272, 256))
COLS = 2
ICH = 4


def kernel(amp_hbm, am, int_hbm, im, occ, vir, out,
           amp_v, int_v, own, pieces, dec, int_t, part, relay, roots, rows_in,
           amp_sem, int_sem, own_send, a_send, a_recv, far_send,
           t_send, t_recv, p_send, y_send, r1_recv, r2_recv, r3_recv):
    row, col = lax.axis_index("row"), lax.axis_index("col")
    z, yh = row // 2, lax.rem(row, 2)
    k, x, yl = lax.rem(col, 2), lax.rem(col // 2, NX), col // (2 * NX)
    z_up, z_dn = lax.rem(z + 1, NZ) * 2 + yh, lax.rem(z + NZ - 1, NZ) * 2 + yh
    x_up = (yl * NX + lax.rem(x + 1, NX)) * 2 + k
    x_dn = (yl * NX + lax.rem(x + NX - 1, NX)) * 2 + k
    core_other = (row, (yl * NX + x) * 2 + 1 - k)
    y_other = (row, ((1 - yl) * NX + x) * 2 + k)
    far_row = z * 2 + 1 - yh
    chip_col = (yl * NX + x) * 2

    def remote(src, dst, send, recv, device):
        return pltpu.make_async_remote_copy(
            src_ref=src, dst_ref=dst, send_sem=send, recv_sem=recv,
            device_id=device, device_id_type=MESH)

    amp_in = pltpu.make_async_copy(amp_hbm, amp_v, amp_sem)
    amp_in.start()
    width = NT * TILE // ICH
    int_in = [pltpu.make_async_copy(int_hbm.at[:, pl.ds(i * width, width)],
                                    int_v.at[:, pl.ds(i * width, width)], int_sem.at[i])
              for i in range(ICH)]
    for c in int_in:
        c.start()

    barrier = pltpu.get_barrier_semaphore()
    for device in ((z_up, col), (z_dn, col), (row, x_up), (row, x_dn), y_other, core_other,
                   (far_row, chip_col), (far_row, chip_col + 1)):
        pl.semaphore_signal(barrier, inc=1, device_id=device, device_id_type=MESH)

    amp_in.wait()
    row_id = lax.broadcasted_iota(jnp.int32, (16, 128), 0)
    for g in range(2):
        codes = jnp.zeros((16, 128), jnp.int32)
        for q in range(2):
            b = g * 2 + q
            count, code = jnp.int32(0), []
            for j in range(NT):
                m = am[b, j]
                count = count + m
                code.append(m * count)
                codes = jnp.where(row_id == q * NT + j, code[j], codes)
            for s in range(KEPT):
                for l in range(2):
                    acc = jnp.zeros((BLK, 128), jnp.bfloat16)
                    for j in range(s, s + KEPT + 1):
                        tile = amp_v[b * BLK:(b + 1) * BLK, j * TILE + l * 128:j * TILE + l * 128 + 128]
                        acc = jnp.where(code[j] == s + 1, tile, acc)
                    at = (s * 2 + l) * HALF + q * BLK
                    own[g, at:at + BLK, :] = acc
        own[g, CODE:CODE + 16, :] = codes.astype(jnp.float32).astype(jnp.bfloat16)

    pl.semaphore_wait(barrier, 8)

    def own_cut(g, u):
        return own.at[g, pl.ds(*CUTS[u]), :]

    def cut(s, g, h, u):
        return pieces.at[s, g, h, pl.ds(*CUTS[u]), :]

    def far(g, u):
        return remote(own_cut(g, u), cut(0, g, k, u), own_send.at[0, g, u],
                      a_recv.at[0, g, k, u], (far_row, chip_col + yh))

    def near(g, u):
        return remote(own_cut(g, u), cut(0, g, k, u), own_send.at[1, g, u],
                      a_recv.at[0, g, k, u], core_other)

    def keep(g, u):
        return pltpu.make_async_copy(own_cut(g, u), cut(0, g, k, u), a_recv.at[0, g, k, u])

    def onward(src, s, g, h, u):
        to = (z_up, col) if g == 0 else (z_dn, col)
        after = lax.rem(s + 1, NZ)
        return remote(src, cut(after, g, h, u), a_send.at[s, g, h, u], a_recv.at[after, g, h, u],
                      to)

    def over(s, g, h, u):
        return remote(cut(s, g, h, u), cut(s, g, h, u), far_send.at[s, g, h, u],
                      a_recv.at[s, g, h, u], (far_row, col))

    def arrived(s, g, h, u):
        remote(cut(s, g, h, u), cut(s, g, h, u), a_send.at[s, g, h, u], a_recv.at[s, g, h, u],
               (z_up, col)).wait_recv()

    home = k == yh
    each = [(u, g) for u in range(2) for g in range(2)]

    @pl.when(home)
    def _():
        for u, g in each:
            onward(own_cut(g, u), 0, g, k, u).start()

    @pl.when(k != yh)
    def _():
        for u, g in each:
            near(g, u).start()

    for u, g in each:
        far(g, u).start()

    @pl.when(home)
    def _():
        for u, g in each:
            keep(g, u).start()

    def goes_on(s):
        return jnp.logical_and(s + 1 < NZ, jnp.logical_or(home, s >= NEAR))

    def goes_over(s):
        return jnp.logical_and(home, jnp.logical_and(s >= 1, s <= NEAR))

    def forward(s, h):
        for u, g in each:
            arrived(s, g, h, u)

            @pl.when(goes_on(s))
            def _():
                onward(cut(s, g, h, u), s, g, h, u).start()

            @pl.when(goes_over(s))
            def _():
                over(s, g, h, u).start()

    def turned(i, device):
        part_rows = pl.ds(pl.multiple_of(k * (NT * TILE) + i * width, width), width)
        return remote(int_t.at[part_rows], int_t.at[part_rows], t_send.at[i], t_recv.at[i], device)

    for i in range(ICH):
        int_in[i].wait()
        for jj in range(width // TILE):
            j = i * (width // TILE) + jj
            for a in range(4):
                tile = int_v[a * TILE:(a + 1) * TILE, j * TILE:(j + 1) * TILE]
                tile = jnp.where(im[a, j] != 0, tile, jnp.zeros_like(tile))
                at = pl.multiple_of(k * (NT * TILE) + j * TILE, TILE)
                int_t[pl.ds(at, TILE), a * TILE:(a + 1) * TILE] = tile.T
        turned(i, core_other).start()
        if i == 0:
            @pl.when(home)
            def _():
                for u, g in each:
                    arrived(0, g, 1 - k, u)
                    onward(cut(0, g, 1 - k, u), 0, g, 1 - k, u).start()

    @pl.when(home)
    def _():
        for u, g in each:
            arrived(0, g, k, u)

    @pl.when(jnp.logical_not(home))
    def _():
        forward(0, 0)
        forward(0, 1)

    for i in range(ICH):
        turned(i, core_other).wait_recv()

    def root_of(s, g):
        zs = lax.rem(z + NZ - s, NZ) if g == 0 else lax.rem(z + s, NZ)
        xr, yr = lax.rem(zs, NX), zs // NX
        return lax.rem(x + NX - xr, NX), yr

    span = part.shape[2] // COLS

    def side(c):
        return pl.ds(c * span, span)

    def halves(s, g, w, c):
        return part.at[s, pl.ds(g * HALF + w * BLK, BLK), side(c)]

    def compute(s):
        def spread(gh, _):
            g, h = gh // 2, lax.rem(gh, 2)
            for q in range(2):
                for j in range(NT):
                    code = jnp.broadcast_to(
                        pieces[s, g, h, CODE + q * NT + j:CODE + q * NT + j + 1, :], (BLK, 128))
                    for l in range(2):
                        acc = jnp.zeros((BLK, 128), jnp.bfloat16)
                        for t in range(max(0, j - KEPT), min(j, KEPT - 1) + 1):
                            at = (t * 2 + l) * HALF + q * BLK
                            acc = jnp.where(code == jnp.bfloat16(t + 1),
                                            pieces[s, g, h, at:at + BLK, :], acc)
                        to_row = pl.multiple_of(g * HALF + q * BLK, BLK)
                        to_col = pl.multiple_of(h * NT * TILE + j * TILE + l * 128, 128)
                        dec[pl.ds(to_row, BLK), pl.ds(to_col, 128)] = acc
            return 0

        lax.fori_loop(0, 4, spread, 0)
        for n in range(4):
            part[s, :, n * TILE:(n + 1) * TILE] = lax.dot_general(
                dec[...], int_t[:, n * TILE:(n + 1) * TILE], (((1,), (0,)), ((), ())),
                preferred_element_type=jnp.float32)

    def send_half(s, g, w, c, dst, recv, device):
        return remote(halves(s, g, w, c), dst, p_send.at[s, g, w, c], recv, device)

    def to_relay(s, g, w, c, device):
        return send_half(s, g, w, c, relay.at[s * 2 + g, :, side(c)], r1_recv.at[s * 2 + g, c],
                         (row, device))

    def to_root(s, g, w, c, yr, come, device):
        i = g * 2 + yr
        return send_half(s, g, w, c, roots.at[i, come, w, :, side(c)],
                         r2_recv.at[i, come, w, c], (row, device))

    def first(s):
        for g in range(2):
            d, yr = root_of(s, g)

            @pl.when(d == 2)
            def _():
                for c in range(COLS):
                    to_relay(s, g, 0, c, x_dn).start()
                    to_relay(s, g, 1, c, x_up).start()

            @pl.when(d == 1)
            def _():
                for c in range(COLS):
                    to_root(s, g, 1, c, yr, 0, x_dn).start()

            @pl.when(d == 3)
            def _():
                for c in range(COLS):
                    to_root(s, g, 0, c, yr, 1, x_up).start()

    def second(s):
        for g in range(2):
            d, yr = root_of(s, g)

            @pl.when(d == 1)
            def _():
                for c in range(COLS):
                    to_relay(s, g, 0, c, x_dn).wait_recv()
                    halves(s, g, 0, c)[...] += relay[s * 2 + g, :, side(c)]
                    to_root(s, g, 0, c, yr, 0, x_dn).start()

            @pl.when(d == 3)
            def _():
                for c in range(COLS):
                    to_relay(s, g, 1, c, x_up).wait_recv()
                    halves(s, g, 1, c)[...] += relay[s * 2 + g, :, side(c)]
                    to_root(s, g, 1, c, yr, 1, x_up).start()

    def cross(s, g, c):
        whole = part.at[s, pl.ds(g * HALF, HALF), side(c)]
        return remote(whole, rows_in.at[g, :, side(c)], y_send.at[s, g, c], r3_recv.at[g, c],
                      y_other)

    def third(s):
        for g in range(2):
            d, yr = root_of(s, g)

            @pl.when(d == 0)
            def _():
                for c in range(COLS):
                    for w in range(2):
                        for come in range(2):
                            to_root(s, g, w, c, yr, come, x_dn).wait_recv()
                        halves(s, g, w, c)[...] += (roots[g * 2 + yr, 0, w, :, side(c)]
                                                    + roots[g * 2 + yr, 1, w, :, side(c)])

                    @pl.when(yr != yl)
                    def _():
                        cross(s, g, c).start()

    def fourth(s):
        for g in range(2):
            d, yr = root_of(s, g)

            @pl.when(jnp.logical_and(d == 0, yr == yl))
            def _():
                occ_col = jnp.broadcast_to(occ[...], (128, 128)).T
                for c in range(COLS):
                    cross(s, g, c).wait_recv()
                    for n in range(8 // COLS):
                        cols = slice(c * span + n * 128, c * span + (n + 1) * 128)
                        total = part[s, g * HALF:(g + 1) * HALF, cols] + rows_in[g, :, cols]
                        denom = vir[:, cols] - occ_col[g * HALF:(g + 1) * HALF, :]
                        out[g * HALF:(g + 1) * HALF, cols] = (total / denom).astype(jnp.bfloat16)

    def step(t, _):
        @pl.when(t < NZ)
        def _():
            compute(t)
            first(t)

        @pl.when(t + 1 < NZ)
        def _():
            forward(t + 1, 0)

        for lag, job in zip(LAG, (second, third, fourth)):
            @pl.when(jnp.logical_and(t >= lag, t - lag < NZ))
            def _():
                job(t - lag)

        @pl.when(t + 1 < NZ)
        def _():
            forward(t + 1, 1)

        return 0

    lax.fori_loop(0, NZ + LAG[2], step, 0)

    for u, g in each:
        far(g, u).wait_send()

    @pl.when(k != yh)
    def _():
        for u, g in each:
            near(g, u).wait_send()

    for i in range(ICH):
        turned(i, core_other).wait_send()

    def drain(s, _):
        for g in range(2):
            @pl.when(goes_on(s))
            def _():
                for h in range(2):
                    for u in range(2):
                        onward(cut(s, g, h, u), s, g, h, u).wait_send()

            @pl.when(goes_over(s))
            def _():
                for h in range(2):
                    for u in range(2):
                        over(s, g, h, u).wait_send()

            d, yr = root_of(s, g)

            @pl.when(d != 0)
            def _():
                for w in range(2):
                    for c in range(COLS):
                        to_relay(s, g, w, c, x_dn).wait_send()

            @pl.when(jnp.logical_and(d == 0, yr != yl))
            def _():
                for c in range(COLS):
                    cross(s, g, c).wait_send()
        return 0

    lax.fori_loop(0, NZ, drain, 0)


def body(amplitudes, amp_mask, integrals, int_mask, occ_energy, vir_energy):
    nij, ncd = amplitudes.shape
    nab = integrals.shape[0]
    dma = pltpu.SemaphoreType.DMA
    vmem = pl.BlockSpec(memory_space=pltpu.VMEM)
    smem = pl.BlockSpec(memory_space=pltpu.SMEM)
    hbm = pl.BlockSpec(memory_space=pl.ANY)
    return pl.pallas_call(
        kernel,
        out_shape=jax.ShapeDtypeStruct((nij, nab), jnp.bfloat16),
        in_specs=[hbm, smem, hbm, smem, vmem, vmem],
        out_specs=vmem,
        scratch_shapes=[
            pltpu.VMEM((nij, ncd), jnp.bfloat16),
            pltpu.VMEM((nab, ncd), jnp.bfloat16),
            pltpu.VMEM((2, PIECE, 128), jnp.bfloat16),
            pltpu.VMEM((NZ, 2, 2, PIECE, 128), jnp.bfloat16),
            pltpu.VMEM((nij, 2 * ncd), jnp.bfloat16),
            pltpu.VMEM((2 * ncd, nab), jnp.bfloat16),
            pltpu.VMEM((NZ, nij, nab), jnp.float32),
            pltpu.VMEM((2 * NZ, BLK, nab), jnp.float32),
            pltpu.VMEM((4, 2, 2, BLK, nab), jnp.float32),
            pltpu.VMEM((2, HALF, nab), jnp.float32),
            dma, dma((ICH,)), dma((2, 2, 2)), dma((NZ, 2, 2, 2)), dma((NZ, 2, 2, 2)),
            dma((NZ, 2, 2, 2)),
            dma((ICH,)), dma((ICH,)), dma((NZ, 2, 2, COLS)), dma((NZ, 2, COLS)),
            dma((2 * NZ, COLS)), dma((4, 2, 2, COLS)), dma((2, COLS)),
        ],
        compiler_params=pltpu.CompilerParams(
            collective_id=0, has_side_effects=True, vmem_limit_bytes=60 * 1024 * 1024),
    )(amplitudes, amp_mask, integrals, int_mask, occ_energy[None, :], vir_energy[None, :])


def solution(mesh):
    return jax.shard_map(
        body,
        mesh=mesh,
        in_specs=(
            P("row", "col"),
            P("row", "col"),
            P("row", "col"),
            P("row", "col"),
            P("col"),
            P("row"),
        ),
        out_specs=P("col", "row"),
        check_vma=False,
    )
```
